32 devices in a mesh: seq: 8 (over z, y), state: 4 (over x, core).
Axes of the slice: x: 2, y: 2, z: 4, core: 2. Of those that a mesh axis runs over, the one named last changes fastest.
Arguments:
- hidden_in: bfloat16 [4096, 2048], P('seq'), may hold values from -6 to 6
- doc_lengths: int32 [4], replicated, may hold values from 1 to 2048, 4096 in all
- gains: bfloat16 [2, 2048], replicated, may hold values from 0.5 to 1.5
- w_in_x: bfloat16 [2, 2048, 4096], P(None, 'seq', 'state'), may hold values from -0.125 to 0.125
- w_in_z: bfloat16 [2, 2048, 4096], P(None, 'seq', 'state'), may hold values from -0.125 to 0.125
- conv_w: bfloat16 [2, 4, 4096], P(None, None, 'state'), may hold values from -3 to 3
- conv_b: bfloat16 [2, 4096], P(None, 'state'), may hold values from -3 to 3
- w_xp: bfloat16 [2, 160, 4096], P(None, 'seq'), as said below
- w_dt: bfloat16 [2, 128, 4096], P(None, 'seq'), may hold values from -0.5 to 0.5
- dt_b: bfloat16 [2, 4096], replicated, may hold values from -4 to 0
- skip: bfloat16 [2, 4096], P(None, 'state'), may hold values from -4 to 4
- w_out: bfloat16 [2, 2048, 4096], P(None, 'seq', 'state'), may hold values from -0.25 to 0.25
- cotangent: bfloat16 [4096, 2048], P('seq'), may hold values from -6 to 6
Outputs:
- hidden_out: bfloat16 [4096, 2048], P('seq')
- grad_in: float32 [4096, 2048], P('seq')
- grad_gains: float32 [2, 2048], replicated
- grad_in_x: float32 [2, 2048, 4096], P(None, 'seq', 'state')
- grad_in_z: float32 [2, 2048, 4096], P(None, 'seq', 'state')
- grad_conv_w: float32 [2, 4, 4096], P(None, None, 'state')
- grad_conv_b: float32 [2, 4096], P(None, 'state')
- grad_xp: float32 [2, 128, 4096], P(None, 'seq', 'state')
- grad_key_query: float32 [2, 32, 4096], P(None, None, 'state')
- grad_dt: float32 [2, 128, 4096], P(None, 'seq', 'state')
- grad_dt_b: float32 [2, 4096], P(None, 'state')
- grad_skip: float32 [2, 4096], P(None, 'state')
- grad_out: float32 [2, 2048, 4096], P(None, 'seq', 'state')
The draws below stay inside these ranges and needn't reach their ends.
Inputs may be any that keep to these rules, and one draw needn't show every extreme that they name: `doc_lengths`: the 4 lengths sum to 4096, and the longest is exactly 2048. `w_xp`: entries of order 4096 ** -0.5 or smaller.
All inputs are finite; a program needn't handle non-finite values.
Results may differ from the reference program's by a relative error of at most 0.024.
The reference program's roundings to bfloat16 on the way count: a program that leaves them out, or rounds other values in their place, can miss the bound.
Values may be sent and summed in bfloat16 or wider, within the bound.
No kernel may reach another device: no remote copies, remote signals or barrier semaphores. Data moves between devices by JAX's collectives and lax.ppermute only.
A program may use at most 448 MiB of HBM per device.

```python
import math
import jax
import jax.numpy as jnp
import numpy as np
from jax import lax

D = 2048
E = 4096
NST = 16
KW = 4
R = 128
LAYERS = 2
DOCS = 4
LEN = 4096
KQR = 160


def draw_w_xp(key, part):
    base_key, scale_key = jax.random.split(key)
    full_shape = (LAYERS, KQR, E)
    standard = jnp.clip(jax.random.normal(base_key, full_shape, jnp.float32), -5.0, 5.0)
    exponent = jax.random.uniform(scale_key, (LAYERS, KQR, 1), jnp.float32, -1.5, 0.0)
    rows_index = jnp.arange(KQR)[None, :, None]
    key_rows = ((rows_index >= R) & (rows_index < R + NST)).astype(jnp.float32)
    row_scale = jnp.exp(2.3025851 * exponent * key_rows) / math.sqrt(E)
    return (standard * row_scale).astype(jnp.bfloat16)


def block_scale(rng, dims, cuts, smallest, high):
    factor_of = 1.0
    for axis_at, blocks in cuts:
        heights = jax.random.uniform(jax.random.fold_in(jax.random.fold_in(rng, 6), axis_at), (blocks,), jnp.float32, smallest / len(cuts), high / len(cuts))
        factor_of = factor_of * jnp.repeat(jnp.exp(heights), dims[axis_at] // blocks).reshape((-1,) + (1,) * (len(dims) - 1 - axis_at))
    return factor_of


def profile(number_of, total, limit, slope):
    portions = [(1 << 20) // math.isqrt(grade ** slope) + 1 for grade in range(2, number_of + 1)]
    rest, holding = total - limit - (number_of - 1), [1] * (number_of - 1)
    while rest > 0:
        movable = [i for i in range(number_of - 1) if holding[i] < limit]
        mass, left = sum([portions[i] for i in movable]), rest
        for i in movable:
            addition = min(limit - holding[i], max(1, left * portions[i] // mass), rest)
            holding[i] = holding[i] + addition
            rest = rest - addition
    return np.array([limit] + holding)


def ragged_sizes(stream_key, number_of, total, limit, skew):
    if number_of == 2:
        one = jax.random.randint(stream_key, (), max(1, total - limit), min(limit, total - 1) + 1)
        return jnp.stack([one, total - one])
    sizes = jnp.asarray(profile(number_of, total, limit, skew), jnp.int32)
    twos = (number_of - 1) // 2
    donor, taker = sizes[1:1 + 2 * twos:2], sizes[2:2 + 2 * twos:2]
    room = jnp.minimum(donor - 1, limit - taker)
    moved = jax.random.randint(jax.random.fold_in(stream_key, 1), (twos,), 0, 1 << 20) % (room + 1)
    sizes = sizes.at[1:1 + 2 * twos:2].set(donor - moved).at[2:2 + 2 * twos:2].set(taker + moved)
    return sizes[jax.random.permutation(jax.random.fold_in(stream_key, 2), number_of)]


def normal_values(key, extent, width, most, pieces=(), held_as=jnp.bfloat16):
    entries = jax.random.normal(key, extent, jnp.float32) * width
    if len(pieces) > 0:
        entries = block_scale(key, extent, pieces, -0.22, 0.18) * entries
    return jnp.clip(entries, min=-most, max=most).astype(held_as)


def setup_inputs(seed: int = 0) -> dict:
    keys = jax.random.split(jax.random.key(seed), 14)
    hidden_in = normal_values(keys[0], (LEN, D), 1.0, 6.0, ((0, 8),))
    doc_lengths = ragged_sizes(keys[1], DOCS, LEN, LEN // 2, 2).astype(jnp.int32)
    gains = jnp.clip(1.0 + 0.1 * jax.random.normal(keys[2], (LAYERS, D), jnp.float32), 0.5, 1.5).astype(jnp.bfloat16)
    w_in_x = normal_values(keys[3], (LAYERS, D, E), D ** -0.5, 0.125, ((1, 8), (2, 4)))
    w_in_z = normal_values(keys[4], (LAYERS, D, E), D ** -0.5, 0.125, ((1, 8), (2, 4)))
    conv_w = normal_values(keys[5], (LAYERS, KW, E), 0.5, 3.0, ((2, 4),))
    conv_b = normal_values(keys[6], (LAYERS, E), 0.5, 3.0, ((1, 4),))
    w_xp = draw_w_xp(jax.random.fold_in(keys[13], 71), 0)
    w_dt = normal_values(keys[8], (LAYERS, R, E), R ** -0.5, 0.5, ((1, 8),))
    dt_b = jnp.clip(jax.random.uniform(keys[9], (LAYERS, E), jnp.float32, -4.0, 0.0), -4.0, 0.0).astype(jnp.bfloat16)
    skip = normal_values(keys[10], (LAYERS, E), 1.0, 4.0, ((1, 4),))
    w_out = normal_values(keys[11], (LAYERS, D, E), (E // 8) ** -0.5, 0.25, ((1, 8), (2, 4)))
    cotangent = normal_values(keys[12], (LEN, D), 1.0, 6.0, ((0, 8),))
    return dict(hidden_in=hidden_in, doc_lengths=doc_lengths, gains=gains, w_in_x=w_in_x, w_in_z=w_in_z, conv_w=conv_w, conv_b=conv_b, w_xp=w_xp, w_dt=w_dt, dt_b=dt_b, skip=skip, w_out=w_out, cotangent=cotangent)


EPSILON = 1e-05
HIGH = lax.Precision.HIGHEST

@jax.custom_vjp
def low(v):
    return lax.optimization_barrier(v.astype(jnp.bfloat16)).astype(jnp.float32)

@jax.custom_vjp
def low_back(v):
    return v

def low_keep(v):
    return (low(v), None)

def low_pass(kept, grad):
    return (grad,)

def back_keep(v):
    return (v, None)

def back_low(kept, grad):
    return (low(grad),)
low.defvjp(low_keep, low_pass)
low_back.defvjp(back_keep, back_low)

def matmul(left, right):
    return jnp.dot(left, right, precision=HIGH, preferred_element_type=jnp.float32)

def doc_index(points, doc_ends):
    return lax.optimization_barrier(jnp.sum((points[:, None] >= doc_ends[None, :]).astype(jnp.int32), axis=1))

def token_tables(points, doc_lengths):
    doc_ends = jnp.cumsum(doc_lengths).astype(jnp.int32)
    doc_starts = (doc_ends - doc_lengths).astype(jnp.int32)
    keep_mask = 1.0 - jnp.any(points[:, None] == doc_starts[None, :], axis=1).astype(jnp.float32)
    own_doc = doc_index(points, doc_ends)
    tap_list = []
    for offset in range(KW):
        earlier = (points - offset).astype(jnp.int32)
        valid_tap = (earlier >= 0) & (doc_index(earlier, doc_ends) == own_doc)
        tap_list.append(valid_tap.astype(jnp.float32))
    return (keep_mask, jnp.stack(tap_list))

def block_scan(state, inputs):

    def token_step(carried, row_data):
        u_row, rate_row, key_row, query_row, keep_row = row_data
        decay_rate = (1.0 - rate_row[:, None] * (key_row * key_row)[None, :]) * keep_row
        carried = decay_rate * carried + (rate_row * u_row)[:, None] * key_row[None, :]
        return (carried, lax.optimization_barrier(jnp.sum(carried * query_row[None, :], axis=1)))
    return lax.scan(token_step, state, inputs)

def recurrence(u_all, step_rate, key_vals, query_vals, keep_mask):
    length = u_all.shape[0]
    block_rows = 128
    block_count = length // block_rows
    inputs = (u_all.reshape(block_count, block_rows, E), step_rate.reshape(block_count, block_rows, E), key_vals.reshape(block_count, block_rows, NST), query_vals.reshape(block_count, block_rows, NST), keep_mask.reshape(block_count, block_rows))
    initial = jnp.zeros((E, NST), jnp.float32)
    _, outputs = lax.scan(jax.checkpoint(block_scan), initial, inputs)
    return outputs.reshape(length, E)

def layer(hidden, weights, keep_mask, tap_masks):
    norm_gain, weight_x, weight_z, conv_taps, conv_bias, proj_weight, rate_weight, rate_bias, skip_gain, out_weight = weights
    length = hidden.shape[0]
    inv_rms = lax.rsqrt(lax.optimization_barrier(jnp.mean(hidden * hidden, axis=1, keepdims=True)) + EPSILON)
    normed = low(hidden * inv_rms * norm_gain[None, :])
    inner_act = low_back(low(matmul(normed, weight_x)))
    gate_in = low_back(matmul(normed, weight_z))
    conv_pre = jnp.broadcast_to(conv_bias[None, :], inner_act.shape)
    for offset in range(KW):
        shifted = jnp.pad(inner_act, ((offset, 0), (0, 0)))[:length]
        conv_pre = conv_pre + conv_taps[offset][None, :] * shifted * tap_masks[offset][:, None]
    activated = low(jax.nn.silu(conv_pre))
    projected = low_back(matmul(activated, proj_weight.T))
    rate_low = low(projected[:, :R])
    key_vals = projected[:, R:R + NST]
    query_vals = projected[:, R + NST:]
    rate_pre = low_back(matmul(rate_low, rate_weight) + rate_bias[None, :])
    beta_gate = jax.nn.sigmoid(rate_pre)
    key_norm = lax.optimization_barrier(jnp.sum(key_vals * key_vals, axis=1, keepdims=True))
    step_rate = beta_gate / (1.0 + beta_gate * key_norm)
    recurrent = recurrence(activated, step_rate, key_vals, query_vals, keep_mask)
    y_value = low_back(recurrent + skip_gain[None, :] * activated)
    gated_out = low(y_value * jax.nn.silu(gate_in))
    branch = low_back(matmul(gated_out, out_weight.T))
    return hidden + branch

def reference(hidden_in, doc_lengths, gains, w_in_x, w_in_z, conv_w, conv_b, w_xp, w_dt, dt_b, skip, w_out, cotangent):
    points = jnp.arange(LEN, dtype=jnp.int32)
    keep_mask, tap_masks = token_tables(points, doc_lengths.astype(jnp.int32))
    params = tuple((weight_arg.astype(jnp.float32) for weight_arg in (gains, w_in_x, w_in_z, conv_w, conv_b, w_xp, w_dt, dt_b, skip, w_out)))

    def forward(hidden, weights):
        for layer_index in range(LAYERS):
            hidden = layer(hidden, tuple((weight_arg[layer_index] for weight_arg in weights)), keep_mask, tap_masks)
        return hidden
    result, pullback = jax.vjp(forward, hidden_in.astype(jnp.float32), params)
    grad_hidden, grad_params = pullback(cotangent.astype(jnp.float32))
    return (result.astype(jnp.bfloat16), grad_hidden, grad_params[0], grad_params[1], grad_params[2], grad_params[3], grad_params[4], grad_params[5][:, :R], grad_params[5][:, R:], grad_params[6], grad_params[7], grad_params[8], grad_params[9])
```

```python
import functools

import jax
import jax.numpy as jnp
from jax import lax
from jax.experimental import pallas as pl
from jax.experimental.pallas import tpu as pltpu
from jax.sharding import PartitionSpec as P

NST = 16
KW = 4
R = 128
LAYERS = 2
SUB = 8
LANES = 128
WIDE = 256
EPSILON = 1e-05
CONTRACT_ROWS = (((0,), (0,)), ((), ()))
CONTRACT_COLS = (((1,), (1,)), ((), ()))
F32 = jnp.float32
BF16 = jnp.bfloat16
KEEP_COL = 2 * NST
KAPPA_COL = 2 * NST + 1
VMEM_LIMIT = 56 * 1024 * 1024


def ring_cycle(count):
    inner = {8: 2, 16: 4}.get(count, 1)
    outer = count // inner
    if inner == 1:
        return list(range(count))
    path = [(i, 0) for i in range(outer)]
    ascending = True
    for i in reversed(range(outer)):
        columns = range(1, inner) if ascending else range(inner - 1, 0, -1)
        path += [(i, j) for j in columns]
        ascending = not ascending
    return [i * inner + j for i, j in path]


class Ring:
    def __init__(self, count):
        self.count = count
        self.cycle = ring_cycle(count)
        self.forward = [(self.cycle[i], self.cycle[(i + 1) % count]) for i in range(count)]
        self.backward = [(b, a) for a, b in self.forward]
        offsets = [0]
        for j in range(1, count // 2):
            offsets += [-j, j]
        offsets.append(count // 2)
        rows = [None] * count
        for at, device in enumerate(self.cycle):
            rows[device] = [self.cycle[(at + offset) % count] for offset in offsets]
        self.order_table = rows
        inverse = []
        for row in rows:
            back = [0] * count
            for slot, block in enumerate(row):
                back[block] = slot
            inverse.append(back)
        self.inverse_table = inverse

    def fwd(self, value):
        return lax.ppermute(value, "seq", self.forward)

    def bwd(self, value):
        return lax.ppermute(value, "seq", self.backward)

    def gather(self, shard):
        half = shard.shape[0] // 2
        ahead = behind = shard
        parts = [shard]
        for _ in range(1, self.count // 2):
            ahead, behind = self.fwd(ahead), self.bwd(behind)
            parts += [ahead, behind]
        parts += [self.fwd(ahead[:half]), self.bwd(behind[half:])]
        return jnp.concatenate(parts, axis=0)

    def scatter(self, part):
        last = part(self.count - 1)
        half = last.shape[0] // 2
        ahead = self.fwd(last[:half].astype(BF16))
        behind = self.bwd(last[half:].astype(BF16))
        for j in range(self.count // 2 - 1, 0, -1):
            to_ahead, to_behind = part(2 * j), part(2 * j - 1)
            if j == self.count // 2 - 1:
                to_ahead = jnp.concatenate([to_ahead[:half] + ahead.astype(F32), to_ahead[half:]], axis=0)
                to_behind = jnp.concatenate([to_behind[:half], to_behind[half:] + behind.astype(F32)], axis=0)
            else:
                to_ahead = to_ahead + ahead.astype(F32)
                to_behind = to_behind + behind.astype(F32)
            ahead, behind = self.fwd(to_ahead.astype(BF16)), self.bwd(to_behind.astype(BF16))
        return part(0) + ahead.astype(F32) + behind.astype(F32)


def take_blocks(values, order, count, axis):
    width = values.shape[axis] // count
    return jnp.concatenate(
        [lax.dynamic_slice_in_dim(values, order[i] * width, width, axis) for i in range(count)],
        axis=axis,
    )


def shifted(value, axis, steps):
    count = lax.axis_size(axis)
    leading, last = (max(0, -steps), min(count, count - steps))
    return lax.ppermute(value, axis, [(source, source + steps) for source in range(leading, last)])


def later(first, second):
    return (first[0] * second[0], second[0] * first[1] + second[1])


def entering(decay, state, reverse):
    count = lax.axis_size("seq")
    sign = -1 if reverse else 1
    pair = (decay, state)
    near = [jax.tree.map(lambda v: shifted(v, "seq", sign * k), pair) for k in (1, 2, 3)]
    three = later(later(near[2], near[1]), near[0])
    four = later(three, pair)
    span = 4
    result = three
    while span < count:
        result = later(jax.tree.map(lambda v: shifted(v, "seq", sign * span), four), result)
        span += 4
        if span < count:
            continue
    return result[1]


def core_swap(value):
    count = lax.axis_size("state")
    return lax.ppermute(value, "state", [(i, i ^ 1) for i in range(count)])


def chip_shift(value, k):
    count = lax.axis_size("state")
    chips = count // 2
    return lax.ppermute(
        value, "state", [(i, ((i // 2 + k) % chips) * 2 + i % 2) for i in range(count)]
    )


def state_place():
    chips = lax.axis_size("state") // 2
    index = lax.axis_index("state")
    return chips, index % 2, index // 2


def rows_scatter(partial):
    chips, core, chip = state_place()
    half = partial.shape[0] // 2
    away = lax.dynamic_slice_in_dim(partial, (1 - core) * half, half, 0).astype(BF16)
    kept = lax.dynamic_slice_in_dim(partial, core * half, half, 0)
    total = kept + core_swap(away).astype(F32)
    rows = half // chips
    own = lax.dynamic_slice_in_dim(total, chip * rows, rows, 0)
    for k in range(1, chips):
        sent = lax.dynamic_slice_in_dim(total, ((chip + k) % chips) * rows, rows, 0).astype(BF16)
        own = own + chip_shift(sent, k).astype(F32)
    return own


def own_rows(values):
    chips, core, chip = state_place()
    rows = values.shape[0] // (2 * chips)
    return lax.dynamic_slice_in_dim(values, (core * chips + chip) * rows, rows, 0)


def rows_gather(own):
    chips, core, chip = state_place()
    rows = own.shape[0]
    if chips == 2:
        other = chip_shift(own, 1)
        half = jnp.where(
            chip == 0, jnp.concatenate([own, other], axis=0), jnp.concatenate([other, own], axis=0)
        )
    else:
        half = jnp.zeros((rows * chips, own.shape[1]), own.dtype)
        half = lax.dynamic_update_slice_in_dim(half, own, chip * rows, 0)
        for k in range(1, chips):
            half = lax.dynamic_update_slice_in_dim(
                half, chip_shift(own, k), ((chip - k) % chips) * rows, 0
            )
    swapped = core_swap(half)
    return jnp.where(
        core == 0,
        jnp.concatenate([half, swapped], axis=0),
        jnp.concatenate([swapped, half], axis=0),
    )


def state_sum(values):
    count = lax.axis_size("state")
    distance = 1
    while distance < count:
        swap = [(i, i ^ distance) for i in range(count)]
        values = values + lax.ppermute(values, "state", swap)
        distance *= 2
    return values


def spread(column, n):
    return jnp.broadcast_to(column[:, n : n + 1], (SUB, LANES))


def fill_tables(kqm_ref, kb, ab, keepb, qb=None, kapb=None):
    @pl.when(pl.program_id(0) == 0)
    def _():
        def body(step, carry):
            values = kqm_ref[pl.ds(pl.multiple_of(step * SUB, SUB), SUB), :]
            keep = spread(values, KEEP_COL)
            keepb[step] = keep
            if kapb is not None:
                kapb[step] = spread(values, KAPPA_COL)
            for n in range(NST):
                key = spread(values, n)
                kb[step, n] = key
                ab[step, n] = key * key * keep
                if qb is not None:
                    qb[step, n] = spread(values, NST + n)
            return carry

        lax.fori_loop(0, kqm_ref.shape[0] // SUB, body, 0)


def lane_tiles(width):
    return [slice(c * LANES, (c + 1) * LANES) for c in range(width // LANES)]


def pair_rows(i):
    return pl.ds(pl.multiple_of(i * 2 * SUB, 2 * SUB), 2 * SUB)


def step_rows(i, half):
    return pl.ds(pl.multiple_of(i * 2 * SUB + half * SUB, SUB), SUB)


def sigmoid(v):
    return 1.0 / (1.0 + jnp.exp(-v))


def summary_kernel(kqm_ref, pre_ref, u_ref, rate_ref, psub_ref, ssub_ref, ptot_ref, stot_ref, kb, ab, keepb, kapb):
    fill_tables(kqm_ref, kb, ab, keepb, kapb=kapb)
    pairs = pre_ref.shape[0] // (2 * SUB)
    for lanes in lane_tiles(pre_ref.shape[1]):

        def body(i, carry):
            decays, states = list(carry[0]), list(carry[1])
            pre = pre_ref[pair_rows(i), lanes]
            u = u_ref[pair_rows(i), lanes].astype(F32)
            for half in (0, 1):
                step = i * 2 + half
                beta = sigmoid(pre[half * SUB : (half + 1) * SUB])
                rate = beta / (1.0 + beta * kapb[step])
                rate_ref[step_rows(i, half), lanes] = rate
                source = rate * u[half * SUB : (half + 1) * SUB]
                keep = keepb[step]
                for n in range(NST):
                    decay = keep - rate * ab[step, n]
                    decays[n] = decays[n] * decay
                    states[n] = decay * states[n] + source * kb[step, n]
            return tuple(decays), tuple(states)

        ones = tuple(jnp.ones((SUB, LANES), F32) for _ in range(NST))
        zeros = tuple(jnp.zeros((SUB, LANES), F32) for _ in range(NST))
        decays, states = lax.fori_loop(0, pairs, body, (ones, zeros))
        for n in range(NST):
            psub_ref[n, :, lanes] = decays[n]
            ssub_ref[n, :, lanes] = states[n]
    total_decay, total_state = psub_ref[:, 0, :], ssub_ref[:, 0, :]
    for j in range(1, SUB):
        decay = psub_ref[:, j, :]
        total_state = decay * total_state + ssub_ref[:, j, :]
        total_decay = total_decay * decay
    ptot_ref[...] = total_decay
    stot_ref[...] = total_state


def output_kernel(kqm_ref, rate_ref, u_ref, gate_ref, skip_ref, psub_ref, ssub_ref, ein_ref, y_ref, gated_ref, border_ref, kb, ab, keepb, qb):
    fill_tables(kqm_ref, kb, ab, keepb, qb=qb)
    pairs = rate_ref.shape[0] // (2 * SUB)
    entry = ein_ref[...]
    for j in range(SUB):
        border_ref[:, j, :] = entry
        if j + 1 < SUB:
            entry = psub_ref[:, j, :] * entry + ssub_ref[:, j, :]
    tiles = lane_tiles(rate_ref.shape[1])
    skips = [jnp.broadcast_to(skip_ref[:, lanes], (SUB, LANES)) for lanes in tiles]

    def body(i, carry):
        states = [list(c) for c in carry]
        us = [u_ref[pair_rows(i), lanes].astype(F32) for lanes in tiles]
        gates = [gate_ref[pair_rows(i), lanes] for lanes in tiles]
        gated = [[], []]
        for half in (0, 1):
            step = i * 2 + half
            part = slice(half * SUB, (half + 1) * SUB)
            keep = keepb[step]
            rates = [rate_ref[step_rows(i, half), lanes] for lanes in tiles]
            sources = [rates[c] * us[c][part] for c in range(2)]
            totals = [skips[c] * us[c][part] for c in range(2)]
            for n in range(NST):
                key, scale, query = kb[step, n], ab[step, n], qb[step, n]
                for c in range(2):
                    decay = keep - rates[c] * scale
                    states[c][n] = decay * states[c][n] + sources[c] * key
                    totals[c] = totals[c] + states[c][n] * query
            for c, lanes in enumerate(tiles):
                y_ref[step_rows(i, half), lanes] = totals[c]
                gate = gates[c][part]
                gated[c].append(totals[c] * (gate * sigmoid(gate)))
        for c, lanes in enumerate(tiles):
            gated_ref[pair_rows(i), lanes] = jnp.concatenate(gated[c], axis=0).astype(BF16)
        return tuple(tuple(s) for s in states)

    start = tuple(tuple(border_ref[n, :, lanes] for n in range(NST)) for lanes in tiles)
    lax.fori_loop(0, pairs, body, start)


def message_kernel(kqm_ref, rate_ref, dy_ref, psub_ref, msub_ref, mtot_ref, qb, ab, keepb):
    fill_tables(kqm_ref, qb, ab, keepb, qb=qb)
    pairs = rate_ref.shape[0] // (2 * SUB)
    tiles = lane_tiles(rate_ref.shape[1])

    def body(j, carry):
        i = pairs - 1 - j
        messages = [list(c) for c in carry]
        dys = [dy_ref[pair_rows(i), lanes].astype(F32) for lanes in tiles]
        for half in (1, 0):
            step = i * 2 + half
            part = slice(half * SUB, (half + 1) * SUB)
            keep = keepb[step]
            rates = [rate_ref[step_rows(i, half), lanes] for lanes in tiles]
            for n in range(NST):
                scale, query = ab[step, n], qb[step, n]
                for c in range(2):
                    decay = keep - rates[c] * scale
                    messages[c][n] = decay * (dys[c][part] * query + messages[c][n])
        return tuple(tuple(m) for m in messages)

    zeros = tuple(tuple(jnp.zeros((SUB, LANES), F32) for _ in range(NST)) for _ in tiles)
    messages = lax.fori_loop(0, pairs, body, zeros)
    for c, lanes in enumerate(tiles):
        for n in range(NST):
            msub_ref[n, :, lanes] = messages[c][n]
    total = msub_ref[:, SUB - 1, :]
    for j in range(SUB - 2, -1, -1):
        total = psub_ref[:, j, :] * total + msub_ref[:, j, :]
    mtot_ref[...] = total


def gradient_kernel(
    kqm_ref, pre_ref, u_ref, dy_ref, skip_ref, border_ref, psub_ref, msub_ref, min_ref,
    dact_ref, dpre_ref, sums_ref, small_ref,
    kb, ab, keepb, qb, kapb, stored, incoming, dkey, dquery, dkappa,
):
    fill_tables(kqm_ref, kb, ab, keepb, qb=qb, kapb=kapb)
    steps = pre_ref.shape[0] // SUB
    pairs = steps // 2

    @pl.when(pl.program_id(0) == 0)
    def _():
        def clear(step, carry):
            dkappa[step] = jnp.zeros((SUB, LANES), F32)
            for n in range(NST):
                dkey[step, n] = jnp.zeros((SUB, LANES), F32)
                dquery[step, n] = jnp.zeros((SUB, LANES), F32)
            return carry

        lax.fori_loop(0, steps, clear, 0)

    message = min_ref[...]
    for j in range(SUB - 1, -1, -1):
        incoming[:, j, :] = message
        if j > 0:
            message = psub_ref[:, j, :] * message + msub_ref[:, j, :]
    tiles = lane_tiles(pre_ref.shape[1])
    skips = [jnp.broadcast_to(skip_ref[:, lanes], (SUB, LANES)) for lanes in tiles]

    def replay(i, carry):
        states = [list(c) for c in carry]
        pres = [pre_ref[pair_rows(i), lanes] for lanes in tiles]
        us = [u_ref[pair_rows(i), lanes].astype(F32) for lanes in tiles]
        dys = [dy_ref[pair_rows(i), lanes].astype(F32) for lanes in tiles]
        for half in (0, 1):
            step = i * 2 + half
            part = slice(half * SUB, (half + 1) * SUB)
            keep, kappa = keepb[step], kapb[step]
            betas = [sigmoid(pres[c][part]) for c in range(2)]
            rates = [betas[c] / (1.0 + betas[c] * kappa) for c in range(2)]
            sources = [rates[c] * us[c][part] for c in range(2)]
            for n in range(NST):
                key, scale = kb[step, n], ab[step, n]
                total = dquery[step, n]
                for c, lanes in enumerate(tiles):
                    stored[step, n, :, lanes] = states[c][n]
                    decay = keep - rates[c] * scale
                    states[c][n] = decay * states[c][n] + sources[c] * key
                    total = total + dys[c][part] * states[c][n]
                dquery[step, n] = total
        return tuple(tuple(s) for s in states)

    start = tuple(tuple(border_ref[n, :, lanes] for n in range(NST)) for lanes in tiles)
    lax.fori_loop(0, pairs, replay, start)

    def body(j, carry):
        i = pairs - 1 - j
        messages = [list(c) for c in carry[0]]
        skip_sums, pre_sums = list(carry[1]), list(carry[2])
        pres = [pre_ref[pair_rows(i), lanes] for lanes in tiles]
        us = [u_ref[pair_rows(i), lanes].astype(F32) for lanes in tiles]
        dys = [dy_ref[pair_rows(i), lanes].astype(F32) for lanes in tiles]
        d_pres = [[None, None], [None, None]]
        for half in (1, 0):
            step = i * 2 + half
            part = slice(half * SUB, (half + 1) * SUB)
            keep, kappa = keepb[step], kapb[step]
            betas = [sigmoid(pres[c][part]) for c in range(2)]
            inverses = [1.0 / (1.0 + betas[c] * kappa) for c in range(2)]
            rates = [betas[c] * inverses[c] for c in range(2)]
            sources = [rates[c] * us[c][part] for c in range(2)]
            keyed = [jnp.zeros((SUB, LANES), F32) for _ in range(2)]
            faded = [jnp.zeros((SUB, LANES), F32) for _ in range(2)]
            twice = keep + keep
            for n in range(NST):
                key, scale, query = kb[step, n], ab[step, n], qb[step, n]
                rate_part = source_part = None
                for c, lanes in enumerate(tiles):
                    decay = keep - rates[c] * scale
                    grad = dys[c][part] * query + messages[c][n]
                    weighted = grad * stored[step, n, :, lanes]
                    keyed[c] = keyed[c] + key * grad
                    faded[c] = faded[c] + scale * weighted
                    r_w, s_g = rates[c] * weighted, sources[c] * grad
                    rate_part = r_w if rate_part is None else rate_part + r_w
                    source_part = s_g if source_part is None else source_part + s_g
                    messages[c][n] = decay * grad
                dkey[step, n] = dkey[step, n] + (source_part - twice * key * rate_part)
            kappa_part = dkappa[step]
            for c, lanes in enumerate(tiles):
                u, dy = us[c][part], dys[c][part]
                d_rate = u * keyed[c] - faded[c]
                dact_ref[step_rows(i, half), lanes] = rates[c] * keyed[c] + skips[c] * dy
                d_beta = d_rate * inverses[c] * inverses[c]
                kappa_part = kappa_part - d_beta * betas[c] * betas[c]
                d_pre = (d_beta * betas[c] * (1.0 - betas[c])).astype(BF16)
                d_pres[c][half] = d_pre
                pre_sums[c] = pre_sums[c] + d_pre.astype(F32)
                skip_sums[c] = skip_sums[c] + dy * u
            dkappa[step] = kappa_part
        for c, lanes in enumerate(tiles):
            dpre_ref[pair_rows(i), lanes] = jnp.concatenate(d_pres[c], axis=0)
        return tuple(tuple(m) for m in messages), tuple(skip_sums), tuple(pre_sums)

    start = tuple(tuple(incoming[n, :, lanes] for n in range(NST)) for lanes in tiles)
    zeros = tuple(jnp.zeros((SUB, LANES), F32) for _ in tiles)
    _, skip_sums, pre_sums = lax.fori_loop(0, pairs, body, (start, zeros, zeros))
    for c, lanes in enumerate(tiles):
        sums_ref[:SUB, lanes] = skip_sums[c]
        sums_ref[SUB:, lanes] = pre_sums[c]

    @pl.when(pl.program_id(0) == pl.num_programs(0) - 1)
    def _():
        lane = lax.broadcasted_iota(jnp.int32, (SUB, LANES), 1)

        def reduce(step, carry):
            row = pl.ds(pl.multiple_of(step * SUB, SUB), SUB)
            values = kqm_ref[row, :]
            kappa_grad = jnp.sum(dkappa[step], axis=1, keepdims=True)
            out = jnp.zeros((SUB, LANES), F32)
            for n in range(NST):
                key_grad = jnp.sum(dkey[step, n], axis=1, keepdims=True)
                key_grad = key_grad + 2.0 * values[:, n : n + 1] * kappa_grad
                query_grad = jnp.sum(dquery[step, n], axis=1, keepdims=True)
                out = jnp.where(lane == n, key_grad, out)
                out = jnp.where(lane == NST + n, query_grad, out)
            small_ref[row, :] = out
            return carry

        lax.fori_loop(0, steps, reduce, 0)


def table(steps):
    return pltpu.VMEM((steps, NST, SUB, LANES), F32)


def tokens(steps):
    return pltpu.VMEM((steps, SUB, LANES), F32)


def cost(microseconds):
    return pl.CostEstimate(flops=0, transcendentals=0, bytes_accessed=int(microseconds * 3.0e6))


def run(kernel, width, in_specs, out_specs, out_shape, scratch, microseconds, *operands):
    return pl.pallas_call(
        kernel,
        grid=(width // WIDE,),
        in_specs=in_specs,
        out_specs=out_specs,
        out_shape=out_shape,
        scratch_shapes=scratch,
        compiler_params=pltpu.CompilerParams(
            dimension_semantics=("arbitrary",), vmem_limit_bytes=VMEM_LIMIT
        ),
        cost_estimate=cost(microseconds),
    )(*operands)


def whole(rows, columns):
    return pl.BlockSpec((rows, columns), lambda c: (0, 0))


def columns_of(rows):
    return pl.BlockSpec((rows, WIDE), lambda c: (0, c))


SUBS = pl.BlockSpec((NST, SUB, WIDE), lambda c: (0, 0, c))


def shape_of(*dims, dtype=F32):
    return jax.ShapeDtypeStruct(dims, dtype)


def summarize(kqm, pre, u):
    count, width = pre.shape
    steps = count // SUB
    return run(
        summary_kernel,
        width,
        [whole(*kqm.shape), columns_of(count), columns_of(count)],
        [columns_of(count), SUBS, SUBS, columns_of(NST), columns_of(NST)],
        [
            shape_of(count, width),
            shape_of(NST, SUB, width),
            shape_of(NST, SUB, width),
            shape_of(NST, width),
            shape_of(NST, width),
        ],
        [table(steps), table(steps), tokens(steps), tokens(steps)],
        8,
        kqm,
        pre,
        u,
    )


def produce(kqm, rate, u, gate, skip, psub, ssub, entry):
    count, width = rate.shape
    steps = count // SUB
    return run(
        output_kernel,
        width,
        [whole(*kqm.shape)] + [columns_of(count)] * 3 + [columns_of(1), SUBS, SUBS, columns_of(NST)],
        [columns_of(count), columns_of(count), SUBS],
        [shape_of(count, width), shape_of(count, width, dtype=BF16), shape_of(NST, SUB, width)],
        [table(steps), table(steps), tokens(steps), table(steps)],
        10,
        kqm,
        rate,
        u,
        gate,
        skip,
        psub,
        ssub,
        entry,
    )


def send_back(kqm, rate, dy, psub):
    count, width = rate.shape
    steps = count // SUB
    return run(
        message_kernel,
        width,
        [whole(*kqm.shape), columns_of(count), columns_of(count), SUBS],
        [SUBS, columns_of(NST)],
        [shape_of(NST, SUB, width), shape_of(NST, width)],
        [table(steps), table(steps), tokens(steps)],
        7,
        kqm,
        rate,
        dy,
        psub,
    )


def differentiate(kqm, pre, u, dy, skip, border, psub, msub, message):
    count, width = pre.shape
    steps = count // SUB
    return run(
        gradient_kernel,
        width,
        [whole(*kqm.shape)] + [columns_of(count)] * 3 + [columns_of(1), SUBS, SUBS, SUBS, columns_of(NST)],
        [columns_of(count), columns_of(count), columns_of(2 * SUB), whole(count, LANES)],
        [
            shape_of(count, width),
            shape_of(count, width, dtype=BF16),
            shape_of(2 * SUB, width),
            shape_of(count, LANES),
        ],
        [
            table(steps),
            table(steps),
            tokens(steps),
            table(steps),
            tokens(steps),
            pltpu.VMEM((steps, NST, SUB, WIDE), F32),
            pltpu.VMEM((NST, SUB, WIDE), F32),
            table(steps),
            table(steps),
            tokens(steps),
        ],
        30,
        kqm,
        pre,
        u,
        dy,
        skip,
        border,
        psub,
        msub,
        message,
    )


def doc_index(points, doc_ends):
    return jnp.sum((points[:, None] >= doc_ends[None, :]).astype(jnp.int32), axis=1)


def tap_mask(points, doc_ends, offset):
    earlier = points - offset
    valid_tap = (earlier >= 0) & (doc_index(earlier, doc_ends) == doc_index(points, doc_ends))
    return valid_tap.astype(F32)


def to_steps(values):
    count = values.shape[0]
    return jnp.swapaxes(values.reshape((SUB, count // SUB) + values.shape[1:]), 0, 1).reshape(values.shape)


def from_steps(values):
    count = values.shape[0]
    return jnp.swapaxes(values.reshape((count // SUB, SUB) + values.shape[1:]), 0, 1).reshape(values.shape)


def matmul(left, right, dims=(((1,), (0,)), ((), ()))):
    return lax.dot_general(left, right, dims, preferred_element_type=F32)


def normalize(hidden, gain):
    inv_rms = lax.rsqrt(jnp.mean(hidden * hidden, axis=1, keepdims=True) + EPSILON)
    scaled = hidden * inv_rms
    return inv_rms, scaled, (scaled * gain[None, :]).astype(BF16)


def layer_forward(normed, weights, vectors, context):
    weight_x, weight_z, weight_out, proj_weight, rate_weight = weights
    conv_taps, conv_bias, rate_bias, skip_gain = vectors
    keep_mask, tap_now, _ = context
    count = normed.shape[0]
    reach = (KW - 1) * SUB
    inner = matmul(normed, weight_x).astype(BF16)
    width = inner.shape[1]
    tail = inner[count - reach :].reshape(KW - 1, SUB, width)
    received = shifted(tail[:, SUB - 1], "seq", 1)
    margin = jnp.concatenate([received[:, None], tail[:, : SUB - 1]], axis=1).reshape(reach, width)
    extended = jnp.concatenate([margin, inner], axis=0)
    conv_pre = jnp.broadcast_to(conv_bias[None, :], (count, width))
    for offset in range(KW):
        at = reach - SUB * offset
        conv_pre = conv_pre + conv_taps[offset][None, :] * extended[at : at + count].astype(F32) * tap_now[offset][:, None]
    activated = jax.nn.silu(conv_pre).astype(BF16)
    projected = state_sum(matmul(activated, proj_weight, CONTRACT_COLS))
    rate_low = projected[:, :R].astype(BF16)
    keys = projected[:, R : R + NST]
    kappa = jnp.sum(keys * keys, axis=1, keepdims=True)
    kqm = jnp.concatenate([projected[:, R:], keep_mask[:, None], kappa], axis=1)
    pre = matmul(rate_low, rate_weight) + rate_bias[None, :]
    rate, psub, ssub, ptot, stot = summarize(kqm, pre, activated)
    entry = entering(ptot, stot, False)
    gate_in = matmul(normed, weight_z)
    y_value, gated, border = produce(kqm, rate, activated, gate_in, skip_gain[None, :], psub, ssub, entry)
    own = rows_scatter(matmul(gated, weight_out, CONTRACT_COLS))
    return own, (normed, extended, conv_pre, activated, rate_low, kqm, pre, rate, psub, ptot, gate_in, y_value, gated, border)


def layer_backward(ring, grad_branch, saved, weights, vectors, context):
    weight_x, weight_z, weight_out, proj_weight, rate_weight = weights
    conv_taps, conv_bias, rate_bias, skip_gain = vectors
    _, tap_now, tap_next = context
    normed, extended, conv_pre, activated, rate_low, kqm, pre, rate, psub, ptot, gate_in, y_value, gated, border = saved
    count, width = gate_in.shape
    reach = (KW - 1) * SUB
    feature = normed.shape[1] // ring.count

    def block(values, i):
        return values[:, i * feature : (i + 1) * feature]

    grad_gated = matmul(grad_branch, weight_out)
    gate_sig = jax.nn.sigmoid(gate_in)
    grad_y = (grad_gated * (gate_in * gate_sig)).astype(BF16)
    grad_gate = (grad_gated * y_value * gate_sig * (1.0 + gate_in * (1.0 - gate_sig))).astype(BF16)
    msub, mtot = send_back(kqm, rate, grad_y, psub)
    message = entering(ptot, mtot, True)
    grad_out_w = ring.scatter(lambda i: matmul(block(grad_branch, i), gated, CONTRACT_ROWS))
    grad_z_w = ring.scatter(lambda i: matmul(block(normed, i), grad_gate, CONTRACT_ROWS))
    grad_act, grad_pre, sums, small = differentiate(
        kqm, pre, activated, grad_y, skip_gain[None, :], border, psub, msub, message
    )
    grad_skip = jnp.sum(sums[:SUB], axis=0)
    grad_rate_bias = jnp.sum(sums[SUB:], axis=0)
    grad_low = matmul(grad_pre, rate_weight, CONTRACT_COLS)
    grad_projected = state_sum(jnp.concatenate([grad_low, small[:, : 2 * NST]], axis=1)).astype(BF16)
    grad_rate_w = matmul(rate_low, grad_pre, CONTRACT_ROWS)
    grad_proj_w = matmul(grad_projected, activated, CONTRACT_ROWS)
    grad_act = grad_act + matmul(grad_projected, proj_weight)
    conv_sig = jax.nn.sigmoid(conv_pre)
    grad_conv = grad_act * conv_sig * (1.0 + conv_pre * (1.0 - conv_sig))
    grad_conv_bias = jnp.sum(grad_conv, axis=0)
    grad_taps = jnp.stack(
        [
            jnp.sum(
                grad_conv
                * extended[reach - SUB * offset : reach - SUB * offset + count].astype(F32)
                * tap_now[offset][:, None],
                axis=0,
            )
            for offset in range(KW)
        ]
    )
    head = grad_conv[:reach].reshape(KW - 1, SUB, width)
    received = shifted(head[:, 0], "seq", -1)
    margin = jnp.concatenate([head[:, 1:], received[:, None]], axis=1).reshape(reach, width)
    grad_ext = jnp.concatenate([grad_conv, margin], axis=0)
    grad_inner = jnp.zeros((count, width), F32)
    for offset in range(KW):
        at = SUB * offset
        grad_inner = grad_inner + conv_taps[offset][None, :] * grad_ext[at : at + count] * tap_next[offset][:, None]
    grad_inner = grad_inner.astype(BF16)
    grad_normed = rows_scatter(
        matmul(grad_inner, weight_x, CONTRACT_COLS) + matmul(grad_gate, weight_z, CONTRACT_COLS)
    )
    grad_x_w = ring.scatter(lambda i: matmul(block(normed, i), grad_inner, CONTRACT_ROWS))
    matrices = (grad_x_w, grad_z_w, grad_out_w)
    scattered = (grad_proj_w[:R], grad_rate_w)
    vector_sums = (grad_taps, grad_conv_bias, grad_rate_bias, grad_skip, grad_proj_w[R:])
    return grad_normed, matrices, scattered, vector_sums


def per_device(
    ring, hidden_in, doc_lengths, gains, w_in_x, w_in_z, conv_w, conv_b, w_xp, w_dt, dt_b, skip, w_out, cotangent
):
    count = hidden_in.shape[0]
    seq_index = lax.axis_index("seq")
    state_index = lax.axis_index("state")
    width = w_in_x.shape[2]
    seq_count = ring.count
    order = jnp.asarray(ring.order_table, jnp.int32)[seq_index]
    inverse = jnp.asarray(ring.inverse_table, jnp.int32)[seq_index]

    positions = to_steps(seq_index * count + jnp.arange(count, dtype=jnp.int32))
    docs = doc_lengths.shape[0]
    below = jnp.arange(docs)[:, None] >= jnp.arange(docs)[None, :]
    doc_ends = jnp.sum(jnp.where(below, doc_lengths[None, :], 0), axis=1)
    doc_starts = doc_ends - doc_lengths
    keep_mask = 1.0 - jnp.any(positions[:, None] == doc_starts[None, :], axis=1).astype(F32)
    tap_now = [tap_mask(positions, doc_ends, offset) for offset in range(KW)]
    tap_next = [tap_mask(positions + offset, doc_ends, offset) for offset in range(KW)]
    context = (keep_mask, tap_now, tap_next)

    def own_columns(values):
        return lax.dynamic_slice_in_dim(values, state_index * width, width, values.ndim - 1)

    small_rows = jnp.concatenate([own_columns(w_xp), own_columns(w_dt)], axis=1)
    low_rows = w_xp.shape[1]
    small_weights = lax.all_gather(small_rows, "seq", axis=0)
    proj_weights = jnp.swapaxes(small_weights[:, :, :low_rows], 0, 1).reshape(LAYERS, -1, width)
    rate_weights = jnp.swapaxes(small_weights[:, :, low_rows:], 0, 1).reshape(LAYERS, -1, width)
    rate_biases = own_columns(dt_b).astype(F32)

    fetched = []
    for layer in range(LAYERS):
        fetched.append(
            (
                ring.gather(w_in_x[layer]),
                ring.gather(w_in_z[layer]),
                ring.gather(w_out[layer]),
                proj_weights[layer],
                rate_weights[layer],
            )
        )
    vectors = [
        (conv_w[layer].astype(F32), conv_b[layer].astype(F32), rate_biases[layer], skip[layer].astype(F32))
        for layer in range(LAYERS)
    ]
    gain_rows = take_blocks(gains, order, seq_count, 1).astype(F32)

    hidden = to_steps(take_blocks(hidden_in, order, seq_count, 1)).astype(F32)
    normed = normalize(hidden, gain_rows[0])[2]
    own_hidden = own_rows(hidden)
    residuals, stored = [], []
    for layer in range(LAYERS):
        inv_rms, scaled, own_normed = normalize(own_hidden, gain_rows[layer])
        if layer > 0:
            normed = rows_gather(own_normed)
        residuals.append((inv_rms, scaled))
        branch, saved = layer_forward(normed, fetched[layer], vectors[layer], context)
        stored.append(saved)
        own_hidden = own_hidden + branch
    hidden_out = take_blocks(from_steps(rows_gather(own_hidden.astype(BF16))), inverse, seq_count, 1)

    grad_full = to_steps(take_blocks(cotangent, order, seq_count, 1))
    own_grad = own_rows(grad_full).astype(F32)
    matrix_grads, scatter_grads, vector_grads = [None] * LAYERS, [None] * LAYERS, [None] * LAYERS
    for layer in reversed(range(LAYERS)):
        if layer < LAYERS - 1:
            grad_full = rows_gather(own_grad.astype(BF16))
        grad_normed, matrix_grads[layer], scatter_grads[layer], vector_sums = layer_backward(
            ring, grad_full, stored[layer], fetched[layer], vectors[layer], context
        )
        inv_rms, scaled = residuals[layer]
        grad_gain = jnp.sum(grad_normed * scaled, axis=0)
        weighted = grad_normed * gain_rows[layer][None, :]
        own_grad = own_grad + inv_rms * (
            weighted - scaled * jnp.mean(weighted * scaled, axis=1, keepdims=True)
        )
        grad_gain = lax.psum(take_blocks(grad_gain, inverse, seq_count, 0), ("seq", "state"))
        vector_grads[layer] = (grad_gain,) + lax.psum(vector_sums, "seq")
        scatter_grads[layer] = tuple(
            lax.psum_scatter(v, "seq", scatter_dimension=0, tiled=True) for v in scatter_grads[layer]
        )
    grad_in = take_blocks(from_steps(rows_gather(own_grad)), inverse, seq_count, 1)

    def stack(parts, position):
        return jnp.stack([parts[layer][position] for layer in range(LAYERS)])

    return (
        hidden_out,
        grad_in,
        stack(vector_grads, 0),
        stack(matrix_grads, 0),
        stack(matrix_grads, 1),
        stack(vector_grads, 1),
        stack(vector_grads, 2),
        stack(scatter_grads, 0),
        stack(vector_grads, 5),
        stack(scatter_grads, 1),
        stack(vector_grads, 3),
        stack(vector_grads, 4),
        stack(matrix_grads, 2),
    )


def solution(mesh):
    ring = Ring(mesh.shape["seq"])
    return jax.shard_map(
        functools.partial(per_device, ring),
        mesh=mesh,
        in_specs=(
            P("seq", None),
            P(),
            P(),
            P(None, "seq", "state"),
            P(None, "seq", "state"),
            P(None, None, "state"),
            P(None, "state"),
            P(None, "seq", None),
            P(None, "seq", None),
            P(),
            P(None, "state"),
            P(None, "seq", "state"),
            P("seq", None),
        ),
        out_specs=(
            P("seq", None),
            P("seq", None),
            P(),
            P(None, "seq", "state"),
            P(None, "seq", "state"),
            P(None, None, "state"),
            P(None, "state"),
            P(None, "seq", "state"),
            P(None, None, "state"),
            P(None, "seq", "state"),
            P(None, "state"),
            P(None, "state"),
            P(None, "seq", "state"),
        ),
        check_vma=False,
    )
```
